32 devices in a mesh: out: 4 (over y, x), in: 8 (over z, core).
Axes of the slice: x: 2, y: 2, z: 4, core: 2. Of those that a mesh axis runs over, the one named last changes fastest.
Arguments:
- gradients: bfloat16 [1024, 28672], P('out', 'in'), may hold values from -6 to 6
- activations: bfloat16 [1024, 8192], P('in', 'out'), may hold values from -6 to 6
- out_basis: bfloat16 [28672, 14336], P('in', 'out'), may hold values from -0.03125 to 0.03125
- in_basis: bfloat16 [8192, 8192], P('out', 'in'), may hold values from -0.0625 to 0.0625
- eigen_table: float32 [14336, 8192], P('out', 'in'), may hold values from 0.1 to 2
Outputs:
- updated_table: float32 [14336, 8192], P('out', 'in')
The draws below stay inside these ranges and needn't reach their ends.
All inputs are finite; a program needn't handle non-finite values.
Results may differ from the reference program's by a relative error of at most 0.002.
Values may be sent and summed in bfloat16 or wider, within the bound.
A program may use at most 128 MiB of HBM per device.

```python
import math
import jax
import jax.numpy as jnp
from jax import lax

OUT_DIM = 28672
IN_DIM = 8192
EIG_OUT = 14336
LEN = 128
SEQS = 8
TOKENS = 1024


def steps_of(key, dims, shards, smallest, high):
    def one(dim, shards_of):
        steps = jax.random.uniform(jax.random.fold_in(jax.random.fold_in(key, 6), dim), (shards_of,), jnp.float32, smallest / len(shards), high / len(shards))
        return jnp.repeat(jnp.exp(steps), dims[dim] // shards_of).reshape((-1,) + (1,) * (len(dims) - dim - 1))

    gain = one(*shards[0])
    for cut in shards[1:]:
        gain = gain * one(*cut)
    return gain


def bell_draw(own_key, extent, scale, bound, pieces=(), dtype=jnp.bfloat16):
    result = jax.random.normal(own_key, extent, jnp.float32) * scale
    if len(pieces) > 0:
        result = steps_of(own_key, extent, pieces, -0.22, 0.18) * result
    return jnp.clip(result, min=-bound, max=bound).astype(dtype)


def setup_inputs(seed: int = 0) -> dict:
    splits = jax.random.split(jax.random.key(seed), 6)
    gradients = bell_draw(splits[0], (TOKENS, OUT_DIM), 1.0, 6.0, ((0, 4), (1, 8)))
    activations = bell_draw(splits[1], (TOKENS, IN_DIM), 1.0, 6.0, ((0, 8), (1, 4)))
    out_basis = bell_draw(splits[2], (OUT_DIM, EIG_OUT), OUT_DIM ** -0.5, 0.03125, ((0, 8), (1, 4)))
    in_basis = bell_draw(splits[3], (IN_DIM, IN_DIM), IN_DIM ** -0.5, 0.0625, ((0, 4), (1, 8)))
    eigen_table = jnp.clip(jnp.exp(math.log(2.0) - 2.9957323 * jax.random.uniform(splits[4], (EIG_OUT, IN_DIM), jnp.float32) ** steps_of(splits[4], (EIG_OUT, IN_DIM), ((0, 4), (1, 8)), -0.2, 0.2)), 0.1, 2.0)
    return {"gradients": gradients, "activations": activations, "out_basis": out_basis, "in_basis": in_basis, "eigen_table": eigen_table}


def reference(gradients, activations, out_basis, in_basis, eigen_table):
    rotated_grad = jnp.dot(gradients, out_basis, preferred_element_type=jnp.float32).astype(jnp.bfloat16)
    rotated_act = jnp.dot(activations, in_basis, preferred_element_type=jnp.float32).astype(jnp.bfloat16)
    grad_blocks = rotated_grad.reshape(SEQS, LEN, EIG_OUT)
    act_blocks = rotated_act.reshape(SEQS, LEN, IN_DIM)

    def accumulate(total, pair):
        grad_seq, act_seq = pair
        corr = jnp.dot(grad_seq.T, act_seq, preferred_element_type=jnp.float32)
        return total + corr * corr, None

    total, unused = lax.scan(accumulate, jnp.zeros((EIG_OUT, IN_DIM), jnp.float32), (grad_blocks, act_blocks))
    return eigen_table + total / (SEQS * LEN)
```

```python
import functools

import jax
import jax.numpy as jnp
from jax import lax
from jax.experimental import pallas as pl
from jax.experimental.pallas import tpu as pltpu
from jax.sharding import PartitionSpec as P

LEN = 128
BF16 = jnp.bfloat16
F32 = jnp.float32


def dot32(a, b):
    return jnp.dot(a, b, preferred_element_type=F32)


def plain(gradients, activations, out_basis, in_basis, eigen_table):
    grad_whole = lax.all_gather(gradients, "out", axis=0, tiled=True)
    act_whole = lax.all_gather(activations, "in", axis=0, tiled=True)
    grad_share = lax.psum_scatter(dot32(grad_whole, out_basis), "in", scatter_dimension=0, tiled=True).astype(BF16)
    act_share = lax.psum_scatter(dot32(act_whole, in_basis), "out", scatter_dimension=0, tiled=True).astype(BF16)
    rotated_grad = lax.all_gather(grad_share, "in", axis=0, tiled=True)
    rotated_act = lax.all_gather(act_share, "out", axis=0, tiled=True)
    token_count = rotated_grad.shape[0]
    seq_count = token_count // LEN
    grad_blocks = rotated_grad.reshape(seq_count, LEN, rotated_grad.shape[1])
    act_blocks = rotated_act.reshape(seq_count, LEN, rotated_act.shape[1])
    corr = jnp.einsum("stn,stm->snm", grad_blocks, act_blocks, preferred_element_type=F32)
    return eigen_table + jnp.sum(corr * corr, axis=0) / token_count


def pick(x, index, axis):
    return lax.dynamic_index_in_dim(x, index, axis, keepdims=False)


def turn(in_n, d):
    return [(i, (i + 2 * d) % in_n) for i in range(in_n)]


def line_sum(part, in_n):
    chips = in_n // 2
    me = lax.axis_index("in")
    z, core = me // 2, me % 2
    rows, width = part.shape
    blocks = part.reshape(chips, 2, rows // in_n, width)
    swap = [(i, i ^ 1) for i in range(in_n)]
    got = lax.ppermute(pick(blocks, 1 - core, 1), "in", swap)
    mine = pick(blocks, core, 1) + got
    total = pick(mine, z, 0)
    for d in range(1, chips):
        sent = pick(mine, lax.rem(z + d, chips), 0).astype(BF16)
        total = total + lax.ppermute(sent, "in", turn(in_n, d)).astype(F32)
    return total.astype(BF16)


def line_gather(share, in_n):
    chips = in_n // 2
    me = lax.axis_index("in")
    z, core = me // 2, me % 2
    lower, upper = [], []
    a = b = share
    for t in range(chips - 1):
        ups = [(2 * k + c, 2 * k + 2 + c) for k in range(t, chips - 1) for c in range(2)]
        downs = [(in_n - 1 - p, in_n - 1 - q) for p, q in ups]
        a = lax.ppermute(a, "in", ups)
        b = lax.ppermute(b, "in", downs)
        lower.append(a)
        upper.append(b)
    line = jnp.stack(lower[::-1] + [share] + upper)
    half = lax.dynamic_slice_in_dim(line, chips - 1 - z, chips, 0)
    other = lax.ppermute(half, "in", [(i, i ^ 1) for i in range(in_n)])
    both = lax.dynamic_slice_in_dim(jnp.stack([half, other, half], 1), core, 2, 1)
    return both.reshape(share.shape[0] * in_n, share.shape[1])


def corr_kernel(count, token_count, *refs):
    grads, acts, table, out = refs[:count], refs[count : 2 * count], refs[2 * count], refs[-1]
    total = None
    for g, a in zip(grads, acts):
        for s in range(g.shape[0] // LEN):
            rows = pl.ds(s * LEN, LEN)
            corr = lax.dot_general(g[rows, :], a[rows, :], (((0,), (0,)), ((), ())), preferred_element_type=F32)
            total = corr * corr if total is None else total + corr * corr
    out[...] = table[...] + total / token_count


def correct(grads, acts, table, token_count):
    count = len(grads)
    height, width = table.shape
    tile_h = next(t for t in (256, 128, height) if height % t == 0)
    tile_w = next(t for t in (1024, 512, 256, 128, width) if width % t == 0)
    return pl.pallas_call(
        functools.partial(corr_kernel, count, token_count),
        grid=(width // tile_w, height // tile_h),
        in_specs=[pl.BlockSpec((g.shape[0], tile_h), lambda w, h: (0, h)) for g in grads]
        + [pl.BlockSpec((a.shape[0], tile_w), lambda w, h: (0, w)) for a in acts]
        + [pl.BlockSpec((tile_h, tile_w), lambda w, h: (h, w))],
        out_specs=pl.BlockSpec((tile_h, tile_w), lambda w, h: (h, w)),
        out_shape=jax.ShapeDtypeStruct(table.shape, F32),
        compiler_params=pltpu.CompilerParams(dimension_semantics=("arbitrary", "arbitrary")),
        cost_estimate=pl.CostEstimate(
            flops=4 * token_count * height * width, bytes_accessed=8 * height * width, transcendentals=0
        ),
    )(*grads, *acts, table)


def groups_of(out_n):
    return [list(range(out_n // 2)), list(range(out_n // 2, out_n))]


def staged(out_n, in_n, gradients, activations, out_basis, in_basis, eigen_table):
    rows = gradients.shape[0]
    token_count = rows * out_n
    me = lax.axis_index("out")

    def across(x, bit):
        return lax.ppermute(x, "out", [(i, i ^ bit) for i in range(out_n)])

    blocks = [gradients] + [None] * (out_n - 1)
    bits = [1 << k for k in range(out_n.bit_length() - 1)]
    for bit in bits:
        blocks[bit] = across(gradients, bit)
    for j in range(out_n):
        if blocks[j] is None:
            low, high = j & -j, 1 << (j.bit_length() - 1)
            half = rows // 2
            blocks[j] = jnp.concatenate(
                [across(blocks[j ^ low][:half], low), across(blocks[j ^ high][half:], high)], 0
            )
    act_whole = line_gather(activations, in_n)
    act_part = dot32(act_whole, in_basis).reshape(out_n, rows, in_basis.shape[1])

    def swapped(x, j):
        return lax.ppermute(x, "out", [(i, i ^ j) for i in range(out_n)])

    act_sum = pick(act_part, me, 0)
    for j in range(1, out_n):
        act_sum = act_sum + swapped(pick(act_part, me ^ j, 0), j)
    act_share = act_sum.astype(BF16)
    acts = [act_share] + [swapped(act_share, j) for j in range(1, out_n)]
    grads, paired = [], []
    for group in groups_of(out_n):
        block = jnp.concatenate([blocks[j] for j in group], 0) if len(group) > 1 else blocks[group[0]]
        grads.append(line_gather(line_sum(dot32(block, out_basis), in_n), in_n))
        paired.append(jnp.concatenate([acts[j] for j in group], 0) if len(group) > 1 else acts[group[0]])
    return correct(grads, paired, eigen_table, token_count)


def local(out_n, in_n, gradients, *rest):
    rows = gradients.shape[0]
    if rows % LEN == 0 and rows % (16 * in_n) == 0 and in_n % 2 == 0 and out_n & (out_n - 1) == 0:
        return staged(out_n, in_n, gradients, *rest)
    return plain(gradients, *rest)


def solution(mesh):
    return jax.shard_map(
        functools.partial(local, mesh.shape["out"], mesh.shape["in"]),
        mesh=mesh,
        in_specs=(P("out", "in"), P("in", "out"), P("in", "out"), P("out", "in"), P("out", "in")),
        out_specs=P("out", "in"),
        check_vma=False,
    )
```
